32 devices in a mesh: replica: 4 (over y, x), shard: 8 (over z, core).
Axes of the slice: x: 2, y: 2, z: 4, core: 2. Of those that a mesh axis runs over, the one named last changes fastest.
Arguments:
- tokens: bfloat16 [4096, 4096], P(('replica', 'shard')), parts along dimension 0, may hold values from -6 to 6
- queries: bfloat16 [4096, 2048], P(('replica', 'shard')), parts along dimension 0, may hold values from -48 to 48
- values: bfloat16 [4096, 512], P(('replica', 'shard')), parts along dimension 0, may hold values from -6 to 6
- out_grad: bfloat16 [4096, 2048], P(('replica', 'shard')), parts along dimension 0, may hold values from -6 to 6
- w_key: bfloat16 [16384, 512], P(('replica', 'shard')), parts along dimension 0, may hold values from -0.09375 to 0.09375
- norm_gain: bfloat16 [16384], P(('replica', 'shard')), parts along dimension 0, may hold values from 0.5 to 1.5
- key_momentum: float32 [16384, 512], P(('replica', 'shard')), parts along dimension 0, may hold values from -6 to 6
- gain_momentum: float32 [16384], P(('replica', 'shard')), parts along dimension 0, may hold values from -6 to 6
Outputs:
- attended: bfloat16 [4096, 2048], P(('replica', 'shard')), parts along dimension 0
- new_key_weight: bfloat16 [16384, 512], P(('replica', 'shard')), parts along dimension 0
- new_key_momentum: float32 [16384, 512], P(('replica', 'shard')), parts along dimension 0
- new_gain: bfloat16 [16384], P(('replica', 'shard')), parts along dimension 0
- new_gain_momentum: float32 [16384], P(('replica', 'shard')), parts along dimension 0
The draws below stay inside these ranges and needn't reach their ends.
There are 4 independent parts, one for each index of `replica`. The reference program is written for one: setup_inputs(seed, part) draws one part's arguments, and reference() takes and returns one part's arrays. A program takes and returns all parts, laid end to end along the dimension named above; each array names one. Nothing has to cross between parts.
All inputs are finite; a program needn't handle non-finite values.
Results may differ from the reference program's by a relative error of at most 0.02.
Values may be sent and summed in bfloat16 or wider, within the bound.
No kernel may reach another device: no remote copies, remote signals or barrier semaphores. Data moves between devices by JAX's collectives and lax.ppermute only.
A program may use at most 128 MiB of HBM per device.

```python
import math
import jax
import jax.numpy as jnp
from jax import lax

D = 4096
HD = 128
HEADS = 16
KV_HEADS = 4
TOK_DEV = 128
TOKENS = 1024
N_SHARD = 8


def draw_queries(key, part):
    first_key = jax.random.fold_in(jax.random.fold_in(key, 17), 0)
    unit_draw = jax.random.truncated_normal(first_key, -6.0, 6.0, (TOKENS, HEADS * HD), jnp.float32)
    return unit_draw.astype(jnp.bfloat16)


def block_scale(stream_key, extent, cuts, least, largest):
    loudness, own = 1.0, jax.random.fold_in(stream_key, 6)
    for position, parts in cuts:
        heights = jnp.exp(jax.random.uniform(jax.random.fold_in(own, position), (parts,), jnp.float32, least / len(cuts), largest / len(cuts)))
        loudness = loudness * jnp.repeat(heights, extent[position] // parts).reshape([-1 if axis == position else 1 for axis in range(len(extent))])
    return loudness


def bell_draw(own_key, shape, scale, limit, cuts=(), held_as=jnp.bfloat16):
    array = scale * jax.random.normal(own_key, shape, jnp.float32)
    if cuts:
        array = array * block_scale(own_key, shape, cuts, -0.22, 0.18)
    return jnp.clip(array, -limit, limit).astype(held_as)


def setup_inputs(seed: int = 0, part: int = 0) -> dict:
    splits = jax.random.split(jax.random.key(seed), 9)
    part_keys = jax.random.split(jax.random.fold_in(splits[8], part), 9)
    return {
        "tokens": bell_draw(part_keys[0], (TOKENS, D), 1.0, 6.0, ((0, 8),)),
        "queries": draw_queries(jax.random.fold_in(jax.random.fold_in(splits[8], part), 71), part),
        "values": bell_draw(part_keys[2], (TOKENS, KV_HEADS * HD), 1.0, 6.0, ((0, 8),)),
        "out_grad": bell_draw(part_keys[3], (TOKENS, HEADS * HD), 1.0, 6.0, ((0, 8),)),
        "w_key": bell_draw(part_keys[4], (D, KV_HEADS * HD), D ** -0.5, 0.09375, ((0, 8),)),
        "norm_gain": jnp.clip(1.0 + 0.1 * jax.random.normal(part_keys[5], (D,), jnp.float32), 0.5, 1.5).astype(jnp.bfloat16),
        "key_momentum": bell_draw(part_keys[6], (D, KV_HEADS * HD), 1.0, 6.0, ((0, 8),), jnp.float32),
        "gain_momentum": bell_draw(part_keys[7], (D,), 1.0, 6.0, ((0, 8),), jnp.float32),
    }


epsilon = 1e-05
rope_base = 500000.0
inertia = 0.9
step_size = 0.01

def rounded(array_in):
    return lax.optimization_barrier(array_in.astype(jnp.bfloat16)).astype(jnp.float32)

def rotation_tables(positions, head_width):
    half_width = head_width // 2
    exponent = jnp.arange(half_width, dtype=jnp.float32) * (2.0 / head_width)
    frequency = jnp.exp(-math.log(rope_base) * exponent)
    angles = positions.astype(jnp.float32)[:, None] * frequency[None, :]
    return (jnp.cos(angles)[:, None, :], jnp.sin(angles)[:, None, :])

def rotate_keys(raw_rows, cosine, sine_table):
    first_half, second_half = jnp.split(raw_rows, 2, axis=-1)
    return jnp.concatenate([first_half * cosine - second_half * sine_table, second_half * cosine + first_half * sine_table], axis=-1)

def rotate_back(grad_rows, cosine, sine_table):
    first_half, second_half = jnp.split(grad_rows, 2, axis=-1)
    return jnp.concatenate([first_half * cosine + second_half * sine_table, second_half * cosine - first_half * sine_table], axis=-1)

def reference(tokens, queries, values, out_grad, w_key, norm_gain, key_momentum, gain_momentum):
    group_size = HEADS // KV_HEADS
    score_scale = HD ** (-0.5)
    inputs_float = tokens.astype(jnp.float32)
    inverse_rms = lax.rsqrt(lax.optimization_barrier(jnp.mean(inputs_float * inputs_float, axis=1, keepdims=True)) + epsilon)
    normalized = inputs_float * inverse_rms
    normed = (normalized * norm_gain.astype(jnp.float32)[None, :]).astype(jnp.bfloat16)
    raw_keys = jnp.dot(normed, w_key, preferred_element_type=jnp.float32)
    positions = jnp.arange(TOKENS, dtype=jnp.int32)
    cosine, sine_table = rotation_tables(positions, HD)
    key_rows = rotate_keys(raw_keys.reshape(TOKENS, KV_HEADS, HD), cosine, sine_table).astype(jnp.bfloat16)
    key_float = key_rows.astype(jnp.float32)
    value_float = values.reshape(TOKENS, KV_HEADS, HD).astype(jnp.float32)
    query_blocks = queries.reshape(N_SHARD, TOK_DEV, KV_HEADS, group_size, HD)
    grad_blocks = out_grad.reshape(N_SHARD, TOK_DEV, KV_HEADS, group_size, HD)

    def one_block(key_sum, inputs):
        block_number, query_block, grad_block = inputs
        query_float = query_block.astype(jnp.float32)
        grad_float = grad_block.astype(jnp.float32)
        query_pos = block_number * TOK_DEV + jnp.arange(TOK_DEV, dtype=jnp.int32)
        scores = jnp.einsum('tghd,sgd->ghts', query_float, key_float) * score_scale
        allowed = positions[None, :] <= query_pos[:, None]
        scores = jnp.where(allowed[None, None], scores, -jnp.inf)
        row_max = lax.optimization_barrier(jnp.max(scores, axis=-1))
        weights = jnp.exp(scores - row_max[..., None])
        denominator = lax.optimization_barrier(jnp.sum(weights, axis=-1))
        numerator = jnp.einsum('ghts,sgd->tghd', rounded(weights), value_float)
        attended_full = numerator / jnp.transpose(denominator, (2, 0, 1))[..., None]
        delta_rows = jnp.einsum('tghd,tghd->ght', grad_float, attended_full)
        prob_grad = jnp.einsum('tghd,sgd->ghts', grad_float, value_float)
        score_grad = weights / denominator[..., None] * (prob_grad - delta_rows[..., None])
        key_part = jnp.einsum('ghts,tghd->sgd', rounded(score_grad), query_float) * score_scale
        key_sum = key_sum + rounded(key_part)
        return (key_sum, attended_full.reshape(TOK_DEV, HEADS * HD).astype(jnp.bfloat16))
    start_sum = jnp.zeros((TOKENS, KV_HEADS, HD), jnp.float32)
    block_numbers = jnp.arange(N_SHARD, dtype=jnp.int32)
    key_grad, attended_blocks = lax.scan(one_block, start_sum, (block_numbers, query_blocks, grad_blocks))
    attended = attended_blocks.reshape(TOKENS, HEADS * HD)
    raw_grads = rotate_back(key_grad, cosine, sine_table).reshape(TOKENS, KV_HEADS * HD).astype(jnp.bfloat16)
    weight_grad = jnp.dot(normed.T, raw_grads, preferred_element_type=jnp.float32)
    normed_grad = jnp.dot(raw_grads, w_key.T, preferred_element_type=jnp.float32)
    gain_grad = lax.optimization_barrier(jnp.sum(normed_grad * normalized, axis=0))
    new_key_momentum = inertia * key_momentum + weight_grad
    new_key_weight = (w_key.astype(jnp.float32) - step_size * new_key_momentum).astype(jnp.bfloat16)
    new_gain_momentum = inertia * gain_momentum + gain_grad
    new_gain = (norm_gain.astype(jnp.float32) - step_size * new_gain_momentum).astype(jnp.bfloat16)
    return (attended, new_key_weight, new_key_momentum, new_gain, new_gain_momentum)
```

```python
import functools
import math

import jax
import jax.numpy as jnp
from jax import lax
from jax.experimental import pallas as pl
from jax.experimental.pallas import tpu as pltpu
from jax.sharding import PartitionSpec as P


HD = 128


epsilon = 1e-05
rope_base = 500000.0
inertia = 0.9
step_size = 0.01


def rotation_tables(positions, head_width):
    half_width = head_width // 2
    exponent = jnp.arange(half_width, dtype=jnp.float32) * (2.0 / head_width)
    frequency = jnp.exp(-math.log(rope_base) * exponent)
    angles = positions.astype(jnp.float32)[:, None] * frequency[None, :]
    return (jnp.cos(angles)[:, None, :], jnp.sin(angles)[:, None, :])


def rotate_keys(raw_rows, cosine, sine_table):
    first_half, second_half = jnp.split(raw_rows, 2, axis=-1)
    return jnp.concatenate(
        [
            first_half * cosine - second_half * sine_table,
            second_half * cosine + first_half * sine_table,
        ],
        axis=-1,
    )


def rotate_back(grad_rows, cosine, sine_table):
    first_half, second_half = jnp.split(grad_rows, 2, axis=-1)
    return jnp.concatenate(
        [
            first_half * cosine + second_half * sine_table,
            second_half * cosine - first_half * sine_table,
        ],
        axis=-1,
    )


def general_shards(tokens, queries, values, out_grad, w_key, norm_gain, key_momentum, gain_momentum):
    token_rows, model_width = tokens.shape
    key_width = w_key.shape[1]
    head_width = HD
    key_heads = key_width // head_width
    group_size = queries.shape[1] // key_width
    score_scale = head_width ** (-0.5)
    my_index = lax.axis_index("shard")
    first_token = my_index * token_rows
    last_token = first_token + token_rows - 1
    positions = first_token + jnp.arange(token_rows, dtype=jnp.int32)
    cosine, sine_table = rotation_tables(positions, head_width)
    inputs_float = tokens.astype(jnp.float32)
    inverse_rms = lax.rsqrt(jnp.mean(inputs_float * inputs_float, axis=1, keepdims=True) + epsilon)
    normalized = inputs_float * inverse_rms
    weight_rows = lax.all_gather(w_key, "shard", axis=0, tiled=True)
    gain_rows = lax.all_gather(norm_gain, "shard", axis=0, tiled=True)
    scaled = (normalized * gain_rows.astype(jnp.float32)[None, :]).astype(jnp.bfloat16)
    key_sum = jnp.dot(scaled, weight_rows, preferred_element_type=jnp.float32)
    key_local = rotate_keys(key_sum.reshape(token_rows, key_heads, head_width), cosine, sine_table)
    key_local = key_local.reshape(token_rows, key_width).astype(jnp.bfloat16)
    all_keys, all_values = (
        lax.all_gather(key_local, "shard", axis=0, tiled=True),
        lax.all_gather(values, "shard", axis=0, tiled=True),
    )
    total_tokens = all_keys.shape[0]
    query_heads = queries.reshape(token_rows, key_heads, group_size, head_width)
    grad_heads = out_grad.reshape(token_rows, key_heads, group_size, head_width)

    def block_scores(block_keys, block_begin):
        scores = (
            jnp.einsum(
                "tghd,sgd->ghts", query_heads, block_keys, preferred_element_type=jnp.float32
            )
            * score_scale
        )
        key_pos = block_begin + jnp.arange(block_keys.shape[0], dtype=jnp.int32)
        allowed = key_pos[None, :] <= positions[:, None]
        return jnp.where(allowed[None, None], scores, -jnp.inf)

    block_width = math.gcd(total_tokens, 512)
    block_total = total_tokens // block_width
    key_blocks = all_keys.reshape(block_total, block_width, key_heads, head_width)
    value_blocks = all_values.reshape(block_total, block_width, key_heads, head_width)
    block_starts = jnp.arange(block_total, dtype=jnp.int32) * block_width

    def max_pass(running, inputs):
        block_keys, block_begin = inputs

        def live_max():
            return jnp.maximum(running, jnp.max(block_scores(block_keys, block_begin), axis=-1))

        return (lax.cond(block_begin <= last_token, live_max, lambda: running), None)

    max_start = jnp.full((key_heads, group_size, token_rows), -jnp.inf, jnp.float32)
    row_max, unused = lax.scan(max_pass, max_start, (key_blocks, block_starts))

    def sum_pass(running, inputs):
        block_keys, block_values, block_begin = inputs

        def live_sum():
            denominator, numerator = running
            weights = jnp.exp(block_scores(block_keys, block_begin) - row_max[..., None])
            denominator = denominator + jnp.sum(weights, axis=-1)
            numerator = numerator + jnp.einsum(
                "ghts,sgd->tghd",
                weights.astype(jnp.bfloat16),
                block_values,
                preferred_element_type=jnp.float32,
            )
            return (denominator, numerator)

        return (lax.cond(block_begin <= last_token, live_sum, lambda: running), None)

    sum_start = (
        jnp.zeros((key_heads, group_size, token_rows), jnp.float32),
        jnp.zeros((token_rows, key_heads, group_size, head_width), jnp.float32),
    )
    (denominator, numerator), unused = lax.scan(
        sum_pass, sum_start, (key_blocks, value_blocks, block_starts)
    )
    attended_full = numerator / jnp.transpose(denominator, (2, 0, 1))[..., None]
    attended = attended_full.reshape(token_rows, key_width * group_size).astype(jnp.bfloat16)
    delta_rows = jnp.einsum("tghd,tghd->ght", grad_heads.astype(jnp.float32), attended_full)
    row_count = lax.axis_size("shard") * token_rows
    inner_width = math.gcd(row_count, 512)
    inner_total = row_count // inner_width

    def one_block(counter):
        begin_here = counter * inner_width

        def live_term():
            block_keys = lax.dynamic_slice_in_dim(all_keys, begin_here, inner_width, 0).reshape(
                inner_width, key_heads, head_width
            )
            block_values = lax.dynamic_slice_in_dim(all_values, begin_here, inner_width, 0).reshape(
                inner_width, key_heads, head_width
            )
            probs = (
                jnp.exp(block_scores(block_keys, begin_here) - row_max[..., None])
                / denominator[..., None]
            )
            prob_grad = jnp.einsum(
                "tghd,sgd->ghts", grad_heads, block_values, preferred_element_type=jnp.float32
            )
            score_grad = (probs * (prob_grad - delta_rows[..., None])).astype(jnp.bfloat16)
            return (
                jnp.einsum(
                    "ghts,tghd->sgd", score_grad, query_heads, preferred_element_type=jnp.float32
                )
                * score_scale
            )

        def empty_term():
            return jnp.zeros((inner_width, key_heads, head_width), jnp.float32)

        return lax.cond(begin_here <= last_token, live_term, empty_term)

    block_terms = lax.map(one_block, jnp.arange(inner_total, dtype=jnp.int32))
    key_grads = lax.psum_scatter(
        block_terms.reshape(row_count, key_width).astype(jnp.bfloat16),
        "shard",
        scatter_dimension=0,
        tiled=True,
    ).astype(jnp.float32)
    raw_grads = rotate_back(
        key_grads.reshape(token_rows, key_heads, head_width), cosine, sine_table
    )
    raw_grads = raw_grads.reshape(token_rows, key_width).astype(jnp.bfloat16)
    columns = lax.all_to_all(normalized, "shard", split_axis=1, concat_axis=0, tiled=True)
    normed_columns = (columns * norm_gain.astype(jnp.float32)[None, :]).astype(jnp.bfloat16)
    grad_block = lax.all_gather(raw_grads, "shard", axis=0, tiled=True)
    weight_sum = jnp.einsum(
        "td,tk->dk", normed_columns, grad_block, preferred_element_type=jnp.float32
    )
    normed_grad = jnp.einsum("tk,dk->td", grad_block, w_key, preferred_element_type=jnp.float32)
    gain_sum = jnp.sum(normed_grad * columns, axis=0)
    new_key_momentum = inertia * key_momentum + weight_sum
    new_key_weight = (w_key.astype(jnp.float32) - step_size * new_key_momentum).astype(jnp.bfloat16)
    new_gain_momentum = inertia * gain_momentum + gain_sum
    new_gain = (norm_gain.astype(jnp.float32) - step_size * new_gain_momentum).astype(jnp.bfloat16)
    return (attended, new_key_weight, new_key_momentum, new_gain, new_gain_momentum)


VMEM = pl.BlockSpec(memory_space=pltpu.VMEM)
ANY = pl.BlockSpec(memory_space=pl.ANY)
F32 = jnp.float32
BF16 = jnp.bfloat16


def place():
    me = lax.axis_index("shard")
    return lax.div(me, 2), lax.rem(me, 2)


def block_at(index, width):
    return pl.ds(pl.multiple_of(index * width, width), width)


def as_column(row, width):
    return jnp.transpose(jnp.broadcast_to(row, (width, row.shape[1])))


def call(kernel, name, out_shape, in_specs, out_specs, scratch=(), flops=0, nbytes=0, exps=0):
    return pl.pallas_call(
        kernel,
        out_shape=out_shape,
        in_specs=in_specs,
        out_specs=out_specs,
        scratch_shapes=list(scratch),
        name=name,
        compiler_params=pltpu.CompilerParams(vmem_limit_bytes=60 * 1024 * 1024),
        cost_estimate=pl.CostEstimate(flops=flops, bytes_accessed=nbytes, transcendentals=exps),
    )


def shape(dims, dtype):
    return jax.ShapeDtypeStruct(dims, dtype)


def split_kernel(chips, x_ref, *refs):
    outs, r_ref, sem = refs[:chips], refs[chips], refs[chips + 1]
    z, unused = place()
    width = x_ref.shape[1] // chips
    copies = []
    for k in range(chips):
        copy = pltpu.make_async_copy(x_ref.at[:, block_at(z ^ k, width)], outs[k], sem.at[k])
        copy.start()
        copies.append(copy)
    x = x_ref[...].astype(F32)
    r = lax.rsqrt(jnp.mean(x * x, axis=1, keepdims=True) + epsilon)
    rows = x_ref.shape[0]
    r_ref[...] = jnp.transpose(jnp.broadcast_to(r, (rows, 128)))[:8]
    for copy in copies:
        copy.wait()


def pack_kernel(chips, q_ref, g_ref, v_ref, *refs):
    outs, sem = refs[: chips - 1], refs[chips - 1]
    z, unused = place()
    qw, vw = q_ref.shape[1] // chips, v_ref.shape[1] // chips
    copies = []
    for k in range(1, chips):
        out = outs[k - 1]
        pieces = (
            (q_ref.at[:, block_at(z ^ k, qw)], out.at[:, pl.ds(0, qw)]),
            (g_ref.at[:, block_at(z ^ k, qw)], out.at[:, pl.ds(qw, qw)]),
            (v_ref.at[:, block_at(z ^ k, vw)], out.at[:, pl.ds(2 * qw, vw)]),
        )
        for n, (source, target) in enumerate(pieces):
            copy = pltpu.make_async_copy(source, target, sem.at[k - 1, n])
            copy.start()
            copies.append(copy)
    for copy in copies:
        copy.wait()


def project_kernel(chips, *refs):
    xs, rs = refs[:chips], refs[chips : 2 * chips]
    gain, gain_other, w, w_other = refs[2 * chips : 2 * chips + 4]
    outs, acc = refs[2 * chips + 4 : 3 * chips + 4], refs[3 * chips + 4]
    z, c = place()
    rows, half = xs[0].shape[0], xs[0].shape[1] // 2
    head = acc.shape[1] // chips
    for k in range(chips):
        r = as_column(rs[k][0:1, :], 128)
        r = jnp.concatenate([r] * (half // 128), axis=1)
        total = None
        for side, g_ref, w_ref in ((c, gain, w), (1 - c, gain_other, w_other)):
            normalized = xs[k][:, block_at(side, half)].astype(F32) * r
            normed = (normalized * g_ref[0:1, :].astype(F32)).astype(BF16)
            part = jnp.dot(normed, w_ref[...], preferred_element_type=F32)
            total = part if total is None else total + part
        acc[block_at(z ^ k, rows), :] = total
    for k in range(chips):
        outs[k][...] = acc[:, block_at(z ^ k, head)].astype(outs[k].dtype)


def columns_kernel(chips, *refs):
    xs, keep, send = refs[:chips], refs[chips], refs[chips + 1]
    z, c = place()
    rows, half = xs[0].shape[0], xs[0].shape[1] // 2
    for k in range(chips):
        for side, out in ((c, keep), (1 - c, send)):
            piece = xs[k][:, block_at(side, half)].astype(F32)
            out[:, block_at(z ^ k, rows)] = jnp.transpose(piece).astype(BF16)


def keys_kernel(chips, *refs):
    parts, cosine, sine, out = refs[:chips], refs[chips], refs[chips + 1], refs[chips + 2]
    total = parts[0][...]
    for k in range(1, chips):
        total = total + parts[k][...].astype(F32)
    half = total.shape[1] // 2
    turned = total * cosine[...] + pltpu.roll(total, half, 1) * sine[...]
    out[...] = turned.astype(BF16)


def attention_kernel(chips, group, hd, *refs):
    q_own, g_own, v_own = refs[:3]
    packed = refs[3 : chips + 2]
    keys, keys_other, v_other = refs[chips + 2 : chips + 5]
    atts = refs[chips + 5 : 2 * chips + 5]
    dk_keep, dk_send = refs[2 * chips + 5 : 2 * chips + 7]
    qs, gs, kf, vf, vt, dk, att, sem, out_sem = refs[2 * chips + 7 :]
    z, c = place()
    rows = q_own.shape[0]
    width = group * hd
    copies = []

    def fetch(source, target):
        copy = pltpu.make_async_copy(source, target, sem.at[len(copies)])
        copy.start()
        copies.append(copy)

    for k in range(chips):
        zb = z ^ k
        fetch(keys.at[pl.ds(k * rows, rows), :], kf.at[block_at(2 * k + c, rows), :])
        fetch(keys_other.at[pl.ds(k * rows, rows), :], kf.at[block_at(2 * k + 1 - c, rows), :])
        fetch(v_other.at[pl.ds(k * rows, rows), :], vf.at[block_at(2 * zb + 1 - c, rows), :])
        if k == 0:
            fetch(v_own.at[:, block_at(z, hd)], vf.at[block_at(2 * zb + c, rows), :])
        else:
            source = packed[k - 1].at[:, pl.ds(2 * width, hd)]
            fetch(source, vf.at[block_at(2 * zb + c, rows), :])
        for h in range(group):
            if k == 0:
                fetch(q_own.at[:, block_at(z * group + h, hd)], qs.at[zb, h])
                fetch(g_own.at[:, block_at(z * group + h, hd)], gs.at[zb, h])
            else:
                fetch(packed[k - 1].at[:, pl.ds(h * hd, hd)], qs.at[zb, h])
                fetch(packed[k - 1].at[:, pl.ds(width + h * hd, hd)], gs.at[zb, h])
    for copy in copies:
        copy.wait()
    step = 2 * rows
    for b in range(chips):
        piece = vf[pl.ds(b * step, step), :].astype(F32)
        vt[:, pl.ds(b * step, step)] = jnp.transpose(piece).astype(BF16)
    dk[...] = jnp.zeros_like(dk)
    scale = hd ** (-0.5)
    nt = (((1,), (1,)), ((), ()))
    wide = group * rows
    key_pos = lax.broadcasted_iota(jnp.int32, (step, wide), 0)
    query_pos = lax.rem(lax.broadcasted_iota(jnp.int32, (step, wide), 1), rows) + c * rows
    allowed = key_pos <= query_pos
    for zb in range(chips):
        q = qs[zb].reshape(wide, hd)
        g = gs[zb].reshape(wide, hd)
        scores = []
        for b in range(zb + 1):
            s = lax.dot_general(kf[pl.ds(b * step, step), :], q, nt, preferred_element_type=F32)
            s = s * scale
            if b == zb:
                s = jnp.where(allowed, s, -jnp.inf)
            scores.append(s)
        top = functools.reduce(jnp.maximum, [jnp.max(s, axis=0, keepdims=True) for s in scores])
        exps = [jnp.exp(s - top) for s in scores]
        total = sum(jnp.sum(e, axis=0, keepdims=True) for e in exps)
        numerator = None
        for b in range(zb + 1):
            part = jnp.dot(
                vt[:, pl.ds(b * step, step)], exps[b].astype(BF16), preferred_element_type=F32
            )
            numerator = part if numerator is None else numerator + part
        inverse = 1.0 / total
        full = numerator * inverse
        delta = jnp.sum(jnp.transpose(g.astype(F32)) * full, axis=0, keepdims=True)
        for h in range(group):
            piece = jnp.transpose(full[:, h * rows : (h + 1) * rows])
            att[zb, :, pl.ds(h * hd, hd)] = piece.astype(BF16)
        for b in range(zb + 1):
            p = lax.dot_general(vf[pl.ds(b * step, step), :], g, nt, preferred_element_type=F32)
            ds = ((exps[b] * inverse) * (p - delta)).astype(BF16)
            dk[pl.ds(b * step, step), :] += jnp.dot(ds, q, preferred_element_type=F32)
    outs = []
    for k in range(chips):
        copy = pltpu.make_async_copy(att.at[z ^ k], atts[k], out_sem.at[k])
        copy.start()
        outs.append(copy)
    for b in range(chips):
        target = pl.ds(b * rows, rows)
        dk_keep[target, :] = dk[block_at(2 * b + c, rows), :] * scale
        dk_send[target, :] = dk[block_at(2 * b + 1 - c, rows), :] * scale
    for copy in outs:
        copy.wait()


def grads_kernel(chips, dk_ref, dk_other, cosine, sine, *refs):
    rs, out = refs[:chips], refs[chips]
    z, unused = place()
    rows = dk_ref.shape[0] // chips
    for k in range(chips):
        here = block_at(z ^ k, rows)
        total = dk_ref[here, :] + dk_other[here, :]
        turned = total * cosine[here, :]
        turned = turned - pltpu.roll(total, total.shape[1] // 2, 1) * sine[here, :]
        out[here, :] = (turned * as_column(rs[k][0:1, :], total.shape[1])).astype(BF16)


def update_kernel(chips, *refs):
    keep_t, other_t = refs[:2]
    grads, others = refs[2 : chips + 2], refs[chips + 2 : 2 * chips + 2]
    w, mom, gain, gain_mom = refs[2 * chips + 2 : 2 * chips + 6]
    new_w, new_mom, new_gain, new_gain_mom = refs[2 * chips + 6 :]
    z, unused = place()
    hd = grads[0].shape[1]
    gain_row = gain[0:1, :].astype(F32)
    gain_wide = as_column(gain_row, hd)
    gain_sum = None
    for k in range(chips):
        here = block_at(z ^ k, hd)
        total = jnp.dot(keep_t[...], grads[k][...], preferred_element_type=F32)
        total = total + jnp.dot(other_t[...], others[k][...], preferred_element_type=F32)
        old = w[:, here].astype(F32)
        term = old * total
        gain_sum = term if gain_sum is None else gain_sum + term
        fresh = inertia * mom[:, here] + gain_wide * total
        new_mom[:, here] = fresh
        new_w[:, here] = (old - step_size * fresh).astype(BF16)
    gain_grad = jnp.sum(jnp.transpose(gain_sum), axis=0, keepdims=True)
    fresh = inertia * gain_mom[0:1, :] + gain_grad
    new_gain_mom[...] = fresh
    new_gain[...] = (gain_row - step_size * fresh).astype(BF16)


def join_kernel(chips, *refs):
    z, unused = place()
    width = refs[0].shape[1]
    for k in range(chips):
        refs[chips][:, block_at(z ^ k, width)] = refs[k][...]


def chip_shards(tokens, queries, values, out_grad, w_key, norm_gain, key_momentum, gain_momentum):
    size = lax.axis_size("shard")
    chips = size // 2
    rows, model_width = tokens.shape
    key_width = w_key.shape[1]
    hd = HD
    group = queries.shape[1] // key_width
    width = group * hd
    mine = w_key.shape[0]
    parity_rows = chips * rows
    z, c = place()

    def to_chip(array, k):
        return lax.ppermute(array, "shard", [(j, j ^ (2 * k)) for j in range(size)])

    def to_core(array):
        return lax.ppermute(array, "shard", [(j, j ^ 1) for j in range(size)])

    wide = model_width // chips
    split = call(
        functools.partial(split_kernel, chips),
        "split_tokens",
        [shape((rows, wide), BF16)] * chips + [shape((8, rows), F32)],
        [VMEM],
        [ANY] * chips + [VMEM],
        [pltpu.SemaphoreType.DMA((chips,))],
        flops=4 * rows * model_width,
        nbytes=4 * rows * model_width,
    )(tokens)
    x = [split[0]] + [to_chip(split[k], k) for k in range(1, chips)]
    r = [split[chips]] + [to_chip(split[chips], k) for k in range(1, chips)]
    gain_row = norm_gain.reshape(1, mine)
    gain_other = to_core(gain_row)
    w_other = to_core(w_key)

    packed = call(
        functools.partial(pack_kernel, chips),
        "pack_heads",
        [shape((rows, 2 * width + hd), BF16)] * (chips - 1),
        [VMEM] * 3,
        [ANY] * (chips - 1),
        [pltpu.SemaphoreType.DMA((chips - 1, 3))],
        nbytes=4 * rows * (2 * queries.shape[1] + key_width),
    )(queries, out_grad, values)
    packed = [to_chip(packed[k - 1], k) for k in range(1, chips)]

    blocks = jnp.arange(chips, dtype=jnp.int32) * 2 + c
    positions = blocks[:, None] * rows + jnp.arange(rows, dtype=jnp.int32)[None, :]
    cosine, sine = rotation_tables(positions.reshape(-1), hd)
    cosine = jnp.concatenate([cosine[:, 0], cosine[:, 0]], axis=1)
    sine = jnp.concatenate([-sine[:, 0], sine[:, 0]], axis=1)

    parts = call(
        functools.partial(project_kernel, chips),
        "project_keys",
        [shape((parity_rows, hd), F32)] + [shape((parity_rows, hd), BF16)] * (chips - 1),
        [VMEM] * (2 * chips + 4),
        [VMEM] * chips,
        [pltpu.VMEM((parity_rows, key_width), F32)],
        flops=2 * parity_rows * wide * key_width,
        nbytes=2 * parity_rows * wide + 2 * wide * key_width,
    )(*x, *r, gain_row, gain_other, w_key, w_other)
    parts = [parts[0]] + [to_chip(parts[k], k) for k in range(1, chips)]

    keep_t, send_t = call(
        functools.partial(columns_kernel, chips),
        "token_columns",
        [shape((mine, parity_rows), BF16)] * 2,
        [VMEM] * chips,
        [VMEM] * 2,
        nbytes=4 * parity_rows * wide,
    )(*x)
    other_t = to_core(send_t)

    keys = call(
        functools.partial(keys_kernel, chips),
        "rotate_keys",
        shape((parity_rows, hd), BF16),
        [VMEM] * (chips + 2),
        VMEM,
        nbytes=16 * parity_rows * hd,
    )(*parts, cosine, sine)
    keys_other = to_core(keys)
    v_own = lax.dynamic_slice_in_dim(values, z * hd, hd, 1)
    v_other = to_core(jnp.concatenate([v_own] + [p[:, 2 * width :] for p in packed], axis=0))

    tokens_all = size * rows
    attended = call(
        functools.partial(attention_kernel, chips, group, hd),
        "attention",
        [shape((rows, width), BF16)] * chips + [shape((parity_rows, hd), F32)] * 2,
        [ANY] * (chips + 5),
        [ANY] * chips + [VMEM] * 2,
        [
            pltpu.VMEM((chips, group, rows, hd), BF16),
            pltpu.VMEM((chips, group, rows, hd), BF16),
            pltpu.VMEM((tokens_all, hd), BF16),
            pltpu.VMEM((tokens_all, hd), BF16),
            pltpu.VMEM((hd, tokens_all), BF16),
            pltpu.VMEM((tokens_all, hd), F32),
            pltpu.VMEM((chips, rows, width), BF16),
            pltpu.SemaphoreType.DMA((chips * (4 + 2 * group),)),
            pltpu.SemaphoreType.DMA((chips,)),
        ],
        flops=5 * tokens_all * parity_rows * width,
        nbytes=10 * parity_rows * width,
        exps=parity_rows * group * tokens_all // 2,
    )(queries, out_grad, values, *packed, keys, keys_other, v_other)
    atts, dk_keep, dk_send = attended[:chips], attended[chips], attended[chips + 1]
    dk_other = to_core(dk_send)

    grads = call(
        functools.partial(grads_kernel, chips),
        "rotate_grads",
        shape((parity_rows, hd), BF16),
        [VMEM] * (chips + 4),
        VMEM,
        nbytes=18 * parity_rows * hd,
    )(dk_keep, dk_other, cosine, sine, *r)
    grads = [grads] + [to_chip(grads, k) for k in range(1, chips)]
    others = [to_core(g) for g in grads]
    atts = [atts[0]] + [to_chip(atts[k], k) for k in range(1, chips)]

    new_w, new_mom, new_gain, new_gain_mom = call(
        functools.partial(update_kernel, chips),
        "update",
        [
            shape((mine, key_width), BF16),
            shape((mine, key_width), F32),
            shape((1, mine), BF16),
            shape((1, mine), F32),
        ],
        [VMEM] * (2 * chips + 6),
        [VMEM] * 4,
        flops=2 * tokens_all * mine * key_width,
        nbytes=14 * mine * key_width,
    )(
        keep_t,
        other_t,
        *grads,
        *others,
        w_key,
        key_momentum,
        gain_row,
        gain_momentum.reshape(1, mine),
    )
    result = call(
        functools.partial(join_kernel, chips),
        "join_heads",
        shape((rows, chips * width), BF16),
        [VMEM] * chips,
        VMEM,
        nbytes=4 * rows * chips * width,
    )(*atts)
    return (result, new_w, new_mom, new_gain.reshape(mine), new_gain_mom.reshape(mine))


def shards(tokens, queries, values, out_grad, w_key, *others):
    size = lax.axis_size("shard")
    chips = size // 2
    rows = tokens.shape[0]
    by_chip = (
        size % 2 == 0
        and chips & (chips - 1) == 0
        and w_key.shape[1] == chips * HD
        and rows % 128 == 0
        and w_key.shape[0] % 128 == 0
    )
    body = chip_shards if by_chip else general_shards
    return body(tokens, queries, values, out_grad, w_key, *others)


def solution(mesh):
    in_specs = (
        P(("replica", "shard"), None),
        P(("replica", "shard"), None),
        P(("replica", "shard"), None),
        P(("replica", "shard"), None),
        P(("replica", "shard"), None),
        P(("replica", "shard")),
        P(("replica", "shard"), None),
        P(("replica", "shard")),
    )
    out_specs = (
        P(("replica", "shard"), None),
        P(("replica", "shard"), None),
        P(("replica", "shard"), None),
        P(("replica", "shard")),
        P(("replica", "shard")),
    )
    return jax.shard_map(shards, mesh=mesh, in_specs=in_specs, out_specs=out_specs, check_vma=False)
```
